32 devices in a mesh: gx: 8 (over y, x, core), gy: 4 (over z).
Axes of the slice: x: 2, y: 2, z: 4, core: 2. Of those that a mesh axis runs over, the one named last changes fastest.
Arguments:
- support_funcs: bfloat16 [3072, 16, 128], P('gx', 'gy'), may hold values from -6 to 6
- potential: float32 [16, 128], P('gy'), may hold values from -1 to 1
- kernel: bfloat16 [4, 48, 64, 64], P('gy', 'gx'), may hold values from -0.375 to 0.375
- weighted: bfloat16 [4, 48, 64, 64], P('gy', 'gx'), may hold values from -0.375 to 0.375
- columns: int32 [48, 4], P('gx'), may hold values from 0 to 47, as said below
- regions: int32 [48, 4], P('gx'), may hold values from 0 to 128, as said below
Outputs:
- new_support: float32 [3072, 16, 128], P('gx', 'gy')
- hamiltonian: float32 [4, 48, 64, 64], P('gy', 'gx')
The draws below stay inside these ranges and needn't reach their ends.
Inputs may be any that keep to these rules, and one draw needn't show every extreme that they name: `columns`: the column blocks of row block a are 4 distinct blocks among the 18 blocks owned by gx index a // 6 and its two neighbours, counted cyclically. `regions`: every box spans at least half of 16 along y and half of 128 along z; it starts at 0 in both dimensions where the block index is even and ends at 16 and 128 where it is odd.
All inputs are finite; a program needn't handle non-finite values.
Results may differ from the reference program's by a relative error of at most 0.0011.
Values may be sent and summed in bfloat16 or wider, within the bound.
A program may use at most 64 MiB of HBM per device.

```python
import jax
import jax.numpy as jnp
from jax import lax

B = 64
NBG = 6
CZ = 128
SWEEPS = 3
NB = 48
NORB = 3072
NNZ = 4
NY = 16


def draw_columns(key, part):
    owner_count = NB // NBG
    rows = jnp.arange(NB, dtype=jnp.int32)
    owner = rows // NBG
    keys = jax.random.split(jax.random.fold_in(key, 11), NB)
    picks = jax.vmap(lambda k: jax.random.permutation(k, 3 * NBG))(keys)[:, :NNZ].astype(jnp.int32)
    col_owner = (owner[:, None] - 1 + picks // NBG + owner_count) % owner_count
    return (col_owner * NBG + picks % NBG).astype(jnp.int32)


def draw_regions(key, part):
    key_y, key_z = jax.random.split(jax.random.fold_in(key, 23))
    len_y = jax.random.randint(key_y, (NB,), NY // 2, NY + 1).astype(jnp.int32)
    len_z = jax.random.randint(key_z, (NB,), CZ // 2, CZ + 1).astype(jnp.int32)
    parity = jnp.arange(NB, dtype=jnp.int32) % 2 == 1
    y_from = jnp.where(parity, NY - len_y, 0)
    y_to = jnp.where(parity, NY, len_y)
    z_from = jnp.where(parity, CZ - len_z, 0)
    z_to = jnp.where(parity, CZ, len_z)
    return jnp.stack([y_from, y_to, z_from, z_to], axis=1).astype(jnp.int32)


def levels(key, shape, pieces, smallest, largest):
    level = 1.0
    for axis_at, blocks in pieces:
        heights = jax.random.uniform(jax.random.fold_in(jax.random.fold_in(key, 6), axis_at), (blocks,), jnp.float32, smallest / len(pieces), largest / len(pieces))
        level = level * jnp.repeat(jnp.exp(heights), shape[axis_at] // blocks).reshape((-1,) + (1,) * (len(shape) - 1 - axis_at))
    return level


def normal_values(key, extent, spread, bound, cuts=(), kind=jnp.bfloat16):
    drawn = jax.random.normal(key, extent, jnp.float32) * spread
    if len(cuts) > 0:
        drawn = levels(key, extent, cuts, -0.22, 0.18) * drawn
    return jnp.clip(drawn, min=-bound, max=bound).astype(kind)


def setup_inputs(seed: int = 0) -> dict:
    splits = jax.random.split(jax.random.key(seed), 7)
    support_funcs = normal_values(splits[0], (NORB, NY, CZ), 1.0, 6.0, ((0, 8), (1, 4)))
    potential = jnp.clip(jax.random.uniform(splits[1], (NY, CZ), jnp.float32, -1.0, 1.0) * levels(splits[1], (NY, CZ), ((0, 4),), -0.4, 0.0), -1.0, 1.0)
    kernel = normal_values(splits[2], (NNZ, NB, B, B), (B * NNZ) ** -0.5, 0.375, ((0, 4), (1, 8)))
    weighted = normal_values(splits[3], (NNZ, NB, B, B), (B * NNZ) ** -0.5, 0.375, ((0, 4), (1, 8)))
    columns = draw_columns(jax.random.fold_in(splits[6], 71), 0)
    regions = draw_regions(jax.random.fold_in(splits[6], 71), 0)
    return {"support_funcs": support_funcs, "potential": potential, "kernel": kernel, "weighted": weighted, "columns": columns, "regions": regions}


kinetic_cut = 1.0
step_length = 0.5


def apply_ham(field, potential):
    padded = jnp.pad(field, ((0, 0), (1, 1), (0, 0)))
    beside = padded[:, 2:] + padded[:, :-2] + jnp.roll(field, 1, 2) + jnp.roll(field, -1, 2)
    return -0.5 * (beside - 4.0 * field) + potential[None] * field


def precondition(gradient):
    diag = 1.0 + 2.0 / kinetic_cut
    coef = 0.5 / kinetic_cut
    precond = gradient / diag
    for sweep in range(SWEEPS):
        padded = jnp.pad(precond, ((0, 0), (1, 1), (0, 0)))
        beside = padded[:, 2:] + padded[:, :-2] + jnp.roll(precond, 1, 2) + jnp.roll(precond, -1, 2)
        precond = (gradient + coef * beside) / diag
    return precond


def reference(support_funcs, potential, kernel, weighted, columns, regions):
    phi = support_funcs.astype(jnp.float32)
    applied = apply_ham(phi, potential).astype(jnp.bfloat16)
    cells = NY * CZ
    volume = 1.0 / cells
    applied_blocks = applied.reshape(NB, B, cells)
    phi_blocks = support_funcs.reshape(NB, B, cells)

    def one_row(row):
        picked = columns[row]
        applied_sel = applied_blocks[picked].astype(jnp.float32)
        phi_sel = phi_blocks[picked].astype(jnp.float32)
        kern_rows = kernel[:, row].astype(jnp.float32)
        wght_rows = weighted[:, row].astype(jnp.float32)
        grad_row = jnp.einsum('kij,kjr->ir', kern_rows, applied_sel, precision=lax.Precision.HIGHEST) - jnp.einsum('kij,kjr->ir', wght_rows, phi_sel, precision=lax.Precision.HIGHEST)
        own_block = phi_blocks[row].astype(jnp.float32)
        ham_row = jnp.einsum('ir,kjr->kij', own_block, applied_sel, precision=lax.Precision.HIGHEST) * volume
        return grad_row, ham_row

    grads, hams = lax.map(one_row, jnp.arange(NB, dtype=jnp.int32))
    gradient = grads.reshape(NB * B, NY, CZ)
    precond = precondition(gradient)
    y_index = jnp.arange(NY, dtype=jnp.int32)[None, :, None]
    z_index = jnp.arange(CZ, dtype=jnp.int32)[None, None, :]
    inside = (y_index >= regions[:, 0, None, None]) & (y_index < regions[:, 1, None, None]) & (z_index >= regions[:, 2, None, None]) & (z_index < regions[:, 3, None, None])
    inside = jnp.repeat(inside.astype(jnp.float32), B, axis=0)
    new_support = phi - step_length * (inside * precond)
    return new_support, jnp.transpose(hams, (1, 0, 2, 3))
```

```python
import functools

import jax
import jax.numpy as jnp
from jax import lax
from jax.experimental import pallas as pl
from jax.experimental.pallas import tpu as pltpu
from jax.sharding import PartitionSpec as P

SWEEPS = 3
CHUNK = 2
HALVES = 2
TOP = 32767.0
kinetic_cut = 1.0
step_length = 0.5
f32 = jnp.float32
bf16 = jnp.bfloat16


def remote(src, dst, send, recv, **device):
    return pltpu.make_async_remote_copy(
        src_ref=src,
        dst_ref=dst,
        send_sem=send,
        recv_sem=recv,
        device_id=device,
        device_id_type=pl.DeviceIdType.MESH,
    )


def signal(barrier, **device):
    pl.semaphore_signal(barrier, device_id=device, device_id_type=pl.DeviceIdType.MESH)


def kernel_body(
    n_gx, n_gy, rows_y,
    cols_hbm, regs_hbm, pot_hbm, x_hbm, kern_hbm, wght_hbm,
    out_ref, ham_ref,
    cols_ref, regs_ref, pot_ref, x_ref, kern_ref, wght_ref, wide, phi, app, edges, packs,
    grad, halo_out, halo_in, part, code_out, code_in, top_out, top_in, in_sem,
    x_send, x_recv, e_send, e_recv, f_send, f_recv, k_send, k_recv, g_send, g_recv,
    h_send, h_recv, t_send, t_recv,
):
    gx, gy = lax.axis_index("gx"), lax.axis_index("gy")
    right, left = lax.rem(gx + 1, n_gx), lax.rem(gx + n_gx - 1, n_gx)
    partner = gx + 1 - 2 * lax.rem(gx, 2)
    above, below = jnp.minimum(gy + 1, n_gy - 1), jnp.maximum(gy - 1, 0)
    has_low, has_high = gy > 0, gy < n_gy - 1
    near = 2 - 2 * lax.rem(gx, 2)
    far = 2 - near
    own_slots, nb, size = kern_ref.shape[:3]
    slots = own_slots * n_gy
    depth = x_ref.shape[1]
    brick = size * rows_y
    chunks = nb // CHUNK
    half = size // 2
    volume = 1.0 / (rows_y * n_gy * depth)
    inner, outer = tuple(range(1, rows_y - 1)), (0, rows_y - 1)

    pairs = (
        (x_hbm, x_ref), (kern_hbm, kern_ref), (wght_hbm, wght_ref),
        (pot_hbm, pot_ref), (cols_hbm, cols_ref), (regs_hbm, regs_ref),
    )
    loads = [pltpu.make_async_copy(src, dst, in_sem.at[i]) for i, (src, dst) in enumerate(pairs)]
    for load in loads:
        load.start()
    barrier = pltpu.get_barrier_semaphore()
    signal(barrier, gx=left)
    signal(barrier, gx=right)
    pl.when(has_low)(lambda: signal(barrier, gy=below))
    pl.when(has_high)(lambda: signal(barrier, gy=above))

    def both_sides(action):
        pl.when(has_low)(lambda: action(0))
        pl.when(has_high)(lambda: action(1))

    def beside(side):
        return below if side == 0 else above

    @pl.when(gy == 0)
    def _():
        edges[0] = jnp.zeros(edges.shape[1:], bf16)
        halo_in[0] = jnp.zeros(halo_in.shape[1:], bf16)

    @pl.when(gy == n_gy - 1)
    def _():
        edges[1] = jnp.zeros(edges.shape[1:], bf16)
        halo_in[1] = jnp.zeros(halo_in.shape[1:], bf16)

    def group_at(group):
        return pl.ds(group * nb, nb)

    def x_copy(group, y):
        return remote(
            phi.at[y, group_at(1)], phi.at[y, group_at(group)],
            x_send.at[group, y], x_recv.at[group, y], gx=right if isinstance(group, int) and group == 0 else left,
        )

    def k_copy(up, d, h):
        origin = gy - (d - 1) if up else gy + (d - 1)
        place = pl.ds(jnp.clip(origin, 0, n_gy - 1) * own_slots, own_slots)
        piece = pl.ds(h * (nb // HALVES), nb // HALVES)
        side = 1 if up else 0
        return remote(
            packs.at[place, piece], packs.at[place, piece],
            k_send.at[side, d - 1, h], k_recv.at[side, d - 1, h], gy=beside(side),
        )

    def k_sends(d, h, action):
        pl.when((gy - (d - 1) >= 0) & has_high)(lambda: action(k_copy(True, d, h)))
        pl.when((gy + (d - 1) < n_gy) & has_low)(lambda: action(k_copy(False, d, h)))

    def k_arrived(d, h):
        pl.when(gy - d >= 0)(lambda: k_copy(True, d, h).wait_recv())
        pl.when(gy + d < n_gy)(lambda: k_copy(False, d, h).wait_recv())

    def k_relay(d):
        for h in range(HALVES):
            k_arrived(d - 1, h)
            k_sends(d, h, lambda copy: copy.start())

    def edge_copy(side, group, index):
        y = 0 if side == 0 else rows_y - 1
        return remote(
            phi.at[y, group_at(group)], edges.at[1 - side, group_at(group)],
            e_send.at[side, index], e_recv.at[1 - side, index], gy=beside(side),
        )

    def edges_arrived(group, index):
        both_sides(lambda side: edge_copy(1 - side, group, index).wait_recv())

    def share_copy(side):
        return remote(
            edges.at[side, group_at(1)], edges.at[side, group_at(far)],
            f_send.at[side], f_recv.at[side], gx=partner,
        )

    def apply_rows(group, chosen):
        for i in range(nb):
            p = group * nb + i
            line = {-1: edges[0, p], rows_y: edges[1, p]} if chosen == outer else {}
            for y in range(rows_y):
                line[y] = phi[y, p]
            line = {y: value.astype(f32) for y, value in line.items()}
            for y in chosen:
                center = line[y]
                around = (
                    line[y + 1] + line[y - 1] + pltpu.roll(center, 1, 1) + pltpu.roll(center, depth - 1, 1)
                )
                applied = -0.5 * (around - 4.0 * center) + pot_ref[y : y + 1, :] * center
                app[y, p] = applied.astype(bf16)

    def picks(a):
        start = nb * n_gx + nb - nb * gx
        found = [lax.rem(cols_ref[k, a] + start, nb * n_gx) for k in range(slots)]
        return [jnp.minimum(p, 3 * nb - 1) for p in found]

    def halo_copy(side, i, c):
        y = i if side == 0 else rows_y - SWEEPS + i
        piece = pl.ds(c * CHUNK, CHUNK)
        return remote(
            halo_out.at[y, piece], halo_in.at[1 - side, i, piece],
            g_send.at[side, i, c], g_recv.at[1 - side, i, c], gy=beside(side),
        )

    def gradient_of(chosen):
        for a in range(nb):
            where = picks(a)
            mixing = jnp.concatenate([packs[k, a] for k in range(slots)], axis=1)
            source = jnp.concatenate(
                [
                    jnp.concatenate([v for p in where for v in (app[y, p], phi[y, p])], axis=0)
                    for y in chosen
                ],
                axis=1,
            )
            total = jnp.dot(mixing, source, preferred_element_type=f32)
            for j, y in enumerate(chosen):
                piece = total[:, j * depth : (j + 1) * depth]
                grad[a, y] = piece
                halo_out[y, a] = piece.astype(bf16)
            if a % CHUNK == CHUNK - 1:
                for y in chosen:
                    if y < SWEEPS:
                        pl.when(has_low)(lambda: halo_copy(0, y, a // CHUNK).start())
                    if y >= rows_y - SWEEPS:
                        pl.when(has_high)(
                            lambda: halo_copy(1, y - rows_y + SWEEPS, a // CHUNK).start()
                        )

    def part_of(a):
        def whole(block, p):
            return jnp.concatenate([block[y, p] for y in range(rows_y)], axis=1)

        source = jnp.concatenate([whole(app, p) for p in picks(a)], axis=0)
        block = lax.dot_general(
            whole(phi, nb + a), source, (((1,), (1,)), ((), ())), preferred_element_type=f32
        ) * volume
        for k in range(slots):
            one = block[:, k * size : (k + 1) * size]
            part[k, a] = jnp.concatenate([one[:half], one[half:]], axis=1)

    def split(value):
        return [value[i : i + 8] for i in range(0, half, 8)]

    def encode(s):
        for j in range(own_slots):
            spot = s * own_slots + j
            top = jnp.full((8, 2 * size), 1e-33, f32)
            for a in range(nb):
                for value in split(part[spot, a]):
                    top = jnp.maximum(top, jnp.abs(value))
            top_out[spot] = top
            scale = TOP / top
            for a in range(nb):
                coded = jnp.concatenate([value * scale for value in split(part[spot, a])], axis=0)
                code_out[spot, a] = jnp.round(coded).astype(jnp.int32).astype(jnp.int16)

    def decoded(off, j, a):
        step = top_in[off - 1, j] * (1.0 / TOP)
        coded = code_in[off - 1, j, a].astype(jnp.int32).astype(f32)
        return jnp.concatenate([value * step for value in split(coded)], axis=0)

    def part_copies(off):
        peer = lax.rem(gy + off, n_gy)
        place = pl.ds(peer * own_slots, own_slots)
        return (
            remote(
                top_out.at[place], top_in.at[off - 1], t_send.at[off - 1], t_recv.at[off - 1], gy=peer
            ),
            remote(
                code_out.at[place], code_in.at[off - 1], h_send.at[off - 1], h_recv.at[off - 1], gy=peer
            ),
        )

    def pass_on(off):
        encode(lax.rem(gy + off, n_gy))
        for copy in part_copies(off):
            copy.start()

    diag = 1.0 + 2.0 / kinetic_cut
    coef = 0.5 / kinetic_cut
    low, high = jnp.where(has_low, 1.0, 0.0).astype(f32), jnp.where(has_high, 1.0, 0.0).astype(f32)
    z_index = lax.broadcasted_iota(jnp.int32, (size, depth), 1)

    def finish(a):
        field = [halo_in[0, i, a].astype(f32) for i in range(SWEEPS)]
        field += [grad[a, y] for y in range(rows_y)]
        field += [halo_in[1, i, a].astype(f32) for i in range(SWEEPS)]
        field = [value * (1.0 / diag) for value in field]
        now = list(field)
        for sweep in range(1, SWEEPS + 1):
            later = list(now)
            for i in range(sweep, rows_y + 2 * SWEEPS - sweep):
                around = now[i - 1] + now[i + 1]
                around = around + pltpu.roll(now[i], 1, 1) + pltpu.roll(now[i], depth - 1, 1)
                value = field[i] + (coef / diag) * around
                if i < SWEEPS:
                    value = value * low
                if i >= rows_y + SWEEPS:
                    value = value * high
                later[i] = value
            now = later
        z_in = (z_index >= regs_ref[2, a]) & (z_index < regs_ref[3, a])
        for y in range(rows_y):
            spot = gy * rows_y + y
            y_in = jnp.where((spot >= regs_ref[0, a]) & (spot < regs_ref[1, a]), step_length, 0.0)
            masked = jnp.where(z_in, now[SWEEPS + y] * y_in.astype(f32), 0.0)
            out_ref[pl.ds(a * brick + y, size, stride=rows_y), :] = phi[y, nb + a].astype(f32) - masked

    loads[0].wait()
    wide[...] = x_ref[...].astype(f32)
    for y in outer + inner:
        for a in range(nb):
            phi[y, nb + a] = wide[pl.ds(a * brick + y, size, stride=rows_y), :].astype(bf16)
    loads[1].wait()
    loads[2].wait()
    for j in range(own_slots):
        for a in range(nb):
            packs[gy * own_slots + j, a] = jnp.concatenate([kern_ref[j, a], -wght_ref[j, a]], axis=1)

    pl.semaphore_wait(barrier, 2 + has_low.astype(jnp.int32) + has_high.astype(jnp.int32))
    for y in outer + inner:
        x_copy(0, y).start()
        x_copy(2, y).start()
    for h in range(HALVES):
        k_sends(1, h, lambda copy: copy.start())
    for load in loads[3:]:
        load.wait()
    apply_rows(1, inner)
    if n_gy > 2:
        k_relay(2)
    both_sides(lambda side: edge_copy(side, 1, 0).start())
    for y in range(rows_y):
        x_copy(near, y).wait_recv()
    apply_rows(near, inner)
    for d in range(3, n_gy):
        k_relay(d)
    x_copy(far, outer[0]).wait_recv()
    pl.when(has_low)(lambda: edge_copy(0, far, 1).start())
    x_copy(far, outer[1]).wait_recv()
    pl.when(has_high)(lambda: edge_copy(1, far, 1).start())
    edges_arrived(1, 0)
    both_sides(lambda side: share_copy(side).start())
    apply_rows(1, outer)
    for y in inner:
        x_copy(far, y).wait_recv()
    apply_rows(far, inner)
    for h in range(HALVES):
        k_arrived(n_gy - 1, h)
    gradient_of(inner)
    both_sides(lambda side: share_copy(side).wait_recv())
    apply_rows(near, outer)
    edges_arrived(far, 1)
    apply_rows(far, outer)
    gradient_of(outer)
    for a in range(nb):
        part_of(a)
    for off in range(1, n_gy):
        pass_on(off)
    for c in range(chunks):
        for i in range(SWEEPS):
            both_sides(lambda side: halo_copy(1 - side, i, c).wait_recv())
        for a in range(c * CHUNK, (c + 1) * CHUNK):
            finish(a)

    def take(off):
        for copy in part_copies(off):
            copy.wait_recv()
        for j in range(own_slots):
            for a in range(nb):
                mine = gy * own_slots + j
                part[mine, a] = part[mine, a] + decoded(off, j, a)

    for off in range(1, n_gy):
        take(off)
    for j in range(own_slots):
        for a in range(nb):
            total = part[gy * own_slots + j, a]
            ham_ref[j, a, :half, :] = total[:, :size]
            ham_ref[j, a, half:, :] = total[:, size:]

    for y in range(rows_y):
        x_copy(0, y).wait_send()
        x_copy(2, y).wait_send()
    both_sides(lambda side: share_copy(side).wait_send())
    both_sides(lambda side: edge_copy(side, 1, 0).wait_send())
    both_sides(lambda side: edge_copy(side, far, 1).wait_send())
    for d in range(1, n_gy):
        for h in range(HALVES):
            k_sends(d, h, lambda copy: copy.wait_send())
    for c in range(chunks):
        for i in range(SWEEPS):
            both_sides(lambda side: halo_copy(side, i, c).wait_send())

    for off in range(1, n_gy):
        for copy in part_copies(off):
            copy.wait_send()


def store_body(support_ref, ham_ref, support_out, ham_out, sem):
    copies = [
        pltpu.make_async_copy(support_ref, support_out, sem.at[0]),
        pltpu.make_async_copy(ham_ref, ham_out, sem.at[1]),
    ]
    for copy in copies:
        copy.start()
    for copy in copies:
        copy.wait()


def local(n_gx, n_gy, support_funcs, potential, kernel, weighted, columns, regions):
    own_slots, nb, size = kernel.shape[:3]
    orbitals, rows_y, depth = support_funcs.shape
    slots = own_slots * n_gy
    flat = orbitals * rows_y
    chunks = nb // CHUNK
    vmem = pl.BlockSpec(memory_space=pltpu.VMEM)
    dma = pltpu.SemaphoreType.DMA
    operands = (
        columns.T, regions.T, potential, support_funcs.reshape(flat, depth), kernel, weighted
    )
    planes = (rows_y, 3 * nb, size, depth)
    parts = (slots, nb, size // 2, 2 * size)
    new_support, hamiltonian = pl.pallas_call(
        functools.partial(kernel_body, n_gx, n_gy, rows_y),
        out_shape=(
            jax.ShapeDtypeStruct((flat, depth), f32),
            jax.ShapeDtypeStruct((own_slots, nb, size, size), f32),
        ),
        in_specs=[pl.BlockSpec(memory_space=pltpu.HBM)] * 6,
        out_specs=(vmem, vmem),
        scratch_shapes=[
            pltpu.SMEM((slots, nb), jnp.int32),
            pltpu.SMEM((4, nb), jnp.int32),
            pltpu.VMEM((rows_y, depth), f32),
            pltpu.VMEM((flat, depth), bf16),
            pltpu.VMEM(kernel.shape, bf16),
            pltpu.VMEM(kernel.shape, bf16),
            pltpu.VMEM((flat, depth), f32),
            pltpu.VMEM(planes, bf16),
            pltpu.VMEM(planes, bf16),
            pltpu.VMEM((2, 3 * nb, size, depth), bf16),
            pltpu.VMEM((slots, nb, size, 2 * size), bf16),
            pltpu.VMEM((nb, rows_y, size, depth), f32),
            pltpu.VMEM((rows_y, nb, size, depth), bf16),
            pltpu.VMEM((2, SWEEPS, nb, size, depth), bf16),
            pltpu.VMEM(parts, f32),
            pltpu.VMEM(parts, jnp.int16),
            pltpu.VMEM((n_gy - 1, own_slots) + parts[1:], jnp.int16),
            pltpu.VMEM((slots, 8, 2 * size), f32),
            pltpu.VMEM((n_gy - 1, own_slots, 8, 2 * size), f32),
            dma((6,)),
            dma((3, rows_y)),
            dma((3, rows_y)),
            dma((2, 2)),
            dma((2, 2)),
            dma((2,)),
            dma((2,)),
            dma((2, n_gy - 1, HALVES)),
            dma((2, n_gy - 1, HALVES)),
            dma((2, SWEEPS, chunks)),
            dma((2, SWEEPS, chunks)),
            dma((n_gy - 1,)),
            dma((n_gy - 1,)),
            dma((n_gy - 1,)),
            dma((n_gy - 1,)),
        ],
        compiler_params=pltpu.CompilerParams(
            collective_id=0, has_side_effects=True, vmem_limit_bytes=40 * 1024 * 1024
        ),
    )(*[pltpu.with_memory_space_constraint(v, pltpu.HBM) for v in operands])
    hbm = pl.BlockSpec(memory_space=pltpu.HBM)
    new_support, hamiltonian = pl.pallas_call(
        store_body,
        out_shape=(
            jax.ShapeDtypeStruct(new_support.shape, f32),
            jax.ShapeDtypeStruct(hamiltonian.shape, f32),
        ),
        in_specs=[vmem, vmem],
        out_specs=(hbm, hbm),
        scratch_shapes=[dma((2,))],
        compiler_params=pltpu.CompilerParams(vmem_limit_bytes=8 * 1024 * 1024),
    )(new_support, hamiltonian)
    return (new_support.reshape(orbitals, rows_y, depth), hamiltonian)


def solution(mesh):
    return jax.shard_map(
        functools.partial(local, mesh.shape["gx"], mesh.shape["gy"]),
        mesh=mesh,
        in_specs=(
            P("gx", "gy", None),
            P("gy", None),
            P("gy", "gx", None, None),
            P("gy", "gx", None, None),
            P("gx", None),
            P("gx", None),
        ),
        out_specs=(P("gx", "gy", None), P("gy", "gx", None, None)),
        check_vma=False,
    )
```

```python
import functools

import jax
import jax.numpy as jnp
from jax import lax
from jax.experimental import pallas as pl
from jax.experimental.pallas import tpu as pltpu
from jax.sharding import PartitionSpec as P

SWEEPS = 3
CHUNK = 2
HALVES = 2
TOP = 32767.0
kinetic_cut = 1.0
step_length = 0.5
f32 = jnp.float32
bf16 = jnp.bfloat16


def remote(src, dst, send, recv, **device):
    return pltpu.make_async_remote_copy(
        src_ref=src,
        dst_ref=dst,
        send_sem=send,
        recv_sem=recv,
        device_id=device,
        device_id_type=pl.DeviceIdType.MESH,
    )


def signal(barrier, **device):
    pl.semaphore_signal(barrier, device_id=device, device_id_type=pl.DeviceIdType.MESH)


def kernel_body(
    n_gx, n_gy, rows_y,
    cols_hbm, regs_hbm, pot_hbm, x_hbm, kern_hbm, wght_hbm,
    out_ref, ham_ref,
    cols_ref, regs_ref, pot_ref, x_ref, kern_ref, wght_ref, wide, phi, app, edges, packs,
    grad, halo_out, halo_in, part, code_out, code_in, top_out, top_in, in_sem,
    x_send, x_recv, e_send, e_recv, f_send, f_recv, k_send, k_recv, g_send, g_recv,
    h_send, h_recv, t_send, t_recv, a_send, a_recv,
):
    gx, gy = lax.axis_index("gx"), lax.axis_index("gy")
    right, left = lax.rem(gx + 1, n_gx), lax.rem(gx + n_gx - 1, n_gx)
    odd = lax.rem(gx, 2)
    partner, outside = gx + 1 - 2 * odd, jnp.where(odd == 1, right, left)
    above, below = jnp.minimum(gy + 1, n_gy - 1), jnp.maximum(gy - 1, 0)
    has_low, has_high = gy > 0, gy < n_gy - 1
    near = 2 - 2 * odd
    far = 2 - near
    own_slots, nb, size = kern_ref.shape[:3]
    slots = own_slots * n_gy
    depth = x_ref.shape[1]
    brick = size * rows_y
    chunks = nb // CHUNK
    half = size // 2
    volume = 1.0 / (rows_y * n_gy * depth)
    inner, outer = tuple(range(1, rows_y - 1)), (0, rows_y - 1)

    pairs = (
        (kern_hbm, kern_ref), (wght_hbm, wght_ref), (x_hbm, x_ref),
        (pot_hbm, pot_ref), (cols_hbm, cols_ref), (regs_hbm, regs_ref),
    )
    loads = [pltpu.make_async_copy(src, dst, in_sem.at[i]) for i, (src, dst) in enumerate(pairs)]
    for load in loads:
        load.start()
    barrier = pltpu.get_barrier_semaphore()
    signal(barrier, gx=left)
    signal(barrier, gx=right)
    pl.when(has_low)(lambda: signal(barrier, gy=below))
    pl.when(has_high)(lambda: signal(barrier, gy=above))

    def both_sides(action):
        pl.when(has_low)(lambda: action(0))
        pl.when(has_high)(lambda: action(1))

    def beside(side):
        return below if side == 0 else above

    @pl.when(gy == 0)
    def _():
        edges[0] = jnp.zeros(edges.shape[1:], bf16)
        halo_in[0] = jnp.zeros(halo_in.shape[1:], bf16)

    @pl.when(gy == n_gy - 1)
    def _():
        edges[1] = jnp.zeros(edges.shape[1:], bf16)
        halo_in[1] = jnp.zeros(halo_in.shape[1:], bf16)

    def group_at(group):
        return pl.ds(group * nb, nb)

    def x_copy(group, y):
        return remote(
            phi[y].at[group_at(1)], phi[y].at[group_at(group)],
            x_send.at[group, y], x_recv.at[group, y], gx=right if isinstance(group, int) and group == 0 else left,
        )

    def k_copy(up, d, h):
        origin = gy - (d - 1) if up else gy + (d - 1)
        place = pl.ds(jnp.clip(origin, 0, n_gy - 1) * own_slots, own_slots)
        piece = pl.ds(h * (nb // HALVES), nb // HALVES)
        side = 1 if up else 0
        return remote(
            packs.at[place, piece], packs.at[place, piece],
            k_send.at[side, d - 1, h], k_recv.at[side, d - 1, h], gy=beside(side),
        )

    def k_sends(d, h, action):
        pl.when((gy - (d - 1) >= 0) & has_high)(lambda: action(k_copy(True, d, h)))
        pl.when((gy + (d - 1) < n_gy) & has_low)(lambda: action(k_copy(False, d, h)))

    def k_arrived(d, h):
        pl.when(gy - d >= 0)(lambda: k_copy(True, d, h).wait_recv())
        pl.when(gy + d < n_gy)(lambda: k_copy(False, d, h).wait_recv())

    def k_relay(d):
        for h in range(HALVES):
            k_arrived(d - 1, h)
            k_sends(d, h, lambda copy: copy.start())

    def edge_copy(side, group, index):
        y = 0 if side == 0 else rows_y - 1
        return remote(
            phi[y].at[group_at(group)], edges.at[1 - side, group_at(group)],
            e_send.at[side, index], e_recv.at[1 - side, index], gy=beside(side),
        )

    def edges_arrived(group, index):
        both_sides(lambda side: edge_copy(1 - side, group, index).wait_recv())

    def share_copy(side):
        return remote(
            edges.at[side, group_at(1)], edges.at[side, group_at(far)],
            f_send.at[side], f_recv.at[side], gx=partner,
        )

    def across_copy(side):
        return remote(
            edges.at[side, group_at(1)], edges.at[side, group_at(near)],
            a_send.at[side], a_recv.at[side], gx=outside,
        )

    def across(action):
        pl.when(gy == 0)(lambda: action(1))
        pl.when(gy > 0)(lambda: action(0))

    def across_arrived(side):
        remote(
            edges.at[side, group_at(1)], edges.at[side, group_at(far)],
            a_send.at[side], a_recv.at[side], gx=outside,
        ).wait_recv()

    def apply_rows(group, chosen):
        for i in range(nb):
            p = group * nb + i
            line = {}
            for y in sorted({y + step for y in chosen for step in (-1, 0, 1)}):
                inside = phi[y][p] if 0 <= y < rows_y else edges[0 if y < 0 else 1, p]
                line[y] = inside.astype(f32)
            for y in chosen:
                center = line[y]
                around = (
                    line[y + 1] + line[y - 1] + pltpu.roll(center, 1, 1) + pltpu.roll(center, depth - 1, 1)
                )
                applied = -0.5 * (around - 4.0 * center) + pot_ref[y : y + 1, :] * center
                app[y][p] = applied.astype(bf16)

    def picks(a):
        start = nb * n_gx + nb - nb * gx
        found = [lax.rem(cols_ref[k, a] + start, nb * n_gx) for k in range(slots)]
        return [jnp.minimum(p, 3 * nb - 1) for p in found]

    def halo_copy(side, i, c):
        y = i if side == 0 else rows_y - SWEEPS + i
        piece = pl.ds(c * CHUNK, CHUNK)
        return remote(
            halo_out.at[y, piece], halo_in.at[1 - side, i, piece],
            g_send.at[side, i, c], g_recv.at[1 - side, i, c], gy=beside(side),
        )

    def gradient_of(chosen):
        for a in range(nb):
            where = picks(a)
            mixing = jnp.concatenate([packs[k, a] for k in range(slots)], axis=1)
            source = jnp.concatenate(
                [
                    jnp.concatenate([v for p in where for v in (app[y][p], phi[y][p])], axis=0)
                    for y in chosen
                ],
                axis=1,
            )
            total = jnp.dot(mixing, source, preferred_element_type=f32)
            for j, y in enumerate(chosen):
                piece = total[:, j * depth : (j + 1) * depth]
                grad[a, y] = piece
                halo_out[y, a] = piece.astype(bf16)
            if a % CHUNK == CHUNK - 1:
                for y in chosen:
                    if y < SWEEPS:
                        pl.when(has_low)(lambda: halo_copy(0, y, a // CHUNK).start())
                    if y >= rows_y - SWEEPS:
                        pl.when(has_high)(
                            lambda: halo_copy(1, y - rows_y + SWEEPS, a // CHUNK).start()
                        )

    def part_of(a):
        def whole(block, p):
            return jnp.concatenate([block[y][p] for y in range(rows_y)], axis=1)

        source = jnp.concatenate([whole(app, p) for p in picks(a)], axis=0)
        block = lax.dot_general(
            whole(phi, nb + a), source, (((1,), (1,)), ((), ())), preferred_element_type=f32
        ) * volume
        for k in range(slots):
            one = block[:, k * size : (k + 1) * size]
            part[k, a] = jnp.concatenate([one[:half], one[half:]], axis=1)

    def split(value):
        return [value[i : i + 8] for i in range(0, half, 8)]

    def encode(s):
        for j in range(own_slots):
            spot = s * own_slots + j
            top = jnp.full((8, 2 * size), 1e-33, f32)
            for a in range(nb):
                for value in split(part[spot, a]):
                    top = jnp.maximum(top, jnp.abs(value))
            top_out[spot] = top
            scale = TOP / top
            for a in range(nb):
                coded = jnp.concatenate([value * scale for value in split(part[spot, a])], axis=0)
                code_out[spot, a] = jnp.round(coded).astype(jnp.int32).astype(jnp.int16)

    def decoded(off, j, a):
        step = top_in[off - 1, j] * (1.0 / TOP)
        coded = code_in[off - 1, j, a].astype(jnp.int32).astype(f32)
        return jnp.concatenate([value * step for value in split(coded)], axis=0)

    def part_copies(off):
        peer = lax.rem(gy + off, n_gy)
        place = pl.ds(peer * own_slots, own_slots)
        return (
            remote(
                top_out.at[place], top_in.at[off - 1], t_send.at[off - 1], t_recv.at[off - 1], gy=peer
            ),
            remote(
                code_out.at[place], code_in.at[off - 1], h_send.at[off - 1], h_recv.at[off - 1], gy=peer
            ),
        )

    def pass_on(off):
        encode(lax.rem(gy + off, n_gy))
        for copy in part_copies(off):
            copy.start()

    diag = 1.0 + 2.0 / kinetic_cut
    coef = 0.5 / kinetic_cut
    low, high = jnp.where(has_low, 1.0, 0.0).astype(f32), jnp.where(has_high, 1.0, 0.0).astype(f32)
    z_index = lax.broadcasted_iota(jnp.int32, (size, depth), 1)

    def finish(a):
        field = [halo_in[0, i, a].astype(f32) for i in range(SWEEPS)]
        field += [grad[a, y] for y in range(rows_y)]
        field += [halo_in[1, i, a].astype(f32) for i in range(SWEEPS)]
        field = [value * (1.0 / diag) for value in field]
        now = list(field)
        for sweep in range(1, SWEEPS + 1):
            later = list(now)
            for i in range(sweep, rows_y + 2 * SWEEPS - sweep):
                around = now[i - 1] + now[i + 1]
                around = around + pltpu.roll(now[i], 1, 1) + pltpu.roll(now[i], depth - 1, 1)
                value = field[i] + (coef / diag) * around
                if i < SWEEPS:
                    value = value * low
                if i >= rows_y + SWEEPS:
                    value = value * high
                later[i] = value
            now = later
        z_in = (z_index >= regs_ref[2, a]) & (z_index < regs_ref[3, a])
        for y in range(rows_y):
            spot = gy * rows_y + y
            y_in = jnp.where((spot >= regs_ref[0, a]) & (spot < regs_ref[1, a]), step_length, 0.0)
            masked = jnp.where(z_in, now[SWEEPS + y] * y_in.astype(f32), 0.0)
            out_ref[pl.ds(a * brick + y, size, stride=rows_y), :] = phi[y][nb + a].astype(f32) - masked

    loads[0].wait()
    loads[1].wait()
    for j in range(own_slots):
        for a in range(nb):
            packs[gy * own_slots + j, a] = jnp.concatenate([kern_ref[j, a], -wght_ref[j, a]], axis=1)
    loads[2].wait()
    wide[...] = x_ref[...].astype(f32)

    pl.semaphore_wait(barrier, 2 + has_low.astype(jnp.int32) + has_high.astype(jnp.int32))
    for h in range(HALVES):
        k_sends(1, h, lambda copy: copy.start())
    for y in range(rows_y):
        for a in range(nb):
            phi[y][nb + a] = wide[pl.ds(a * brick + y, size, stride=rows_y), :].astype(bf16)
        x_copy(0, y).start()
        x_copy(2, y).start()
    both_sides(lambda side: edge_copy(side, 1, 0).start())
    for load in loads[3:]:
        load.wait()
    apply_rows(1, inner)
    if n_gy > 2:
        k_relay(2)
    for y in range(rows_y):
        x_copy(near, y).wait_recv()
    apply_rows(near, inner)
    x_copy(far, 0).wait_recv()
    pl.when(gy > 1)(lambda: edge_copy(0, far, 1).start())
    for d in range(3, n_gy):
        k_relay(d)
    edges_arrived(1, 0)
    across(lambda side: across_copy(side).start())
    both_sides(lambda side: share_copy(side).start())
    apply_rows(1, outer)
    both_sides(lambda side: share_copy(side).wait_recv())
    apply_rows(near, outer)
    x_copy(far, 1).wait_recv()
    for y in inner:
        x_copy(far, y + 1).wait_recv()
        apply_rows(far, (y,))
        if y == inner[0]:
            for h in range(HALVES):
                k_arrived(n_gy - 1, h)
        gradient_of((y,))
    pl.when(gy == 0)(lambda: across_arrived(1))
    pl.when((gy > 0) & has_high)(lambda: edge_copy(0, far, 1).wait_recv())
    apply_rows(far, outer[1:])
    gradient_of(outer[1:])
    pl.when(gy > 0)(lambda: across_arrived(0))
    apply_rows(far, outer[:1])
    for a in range(nb):
        part_of(a)
    gradient_of(outer[:1])
    for i in range(1, n_gy):
        pass_on(jnp.where(gy < n_gy // 2, n_gy - i, i))
    for c in range(chunks):
        for i in range(SWEEPS):
            both_sides(lambda side: halo_copy(1 - side, i, c).wait_recv())
        for a in range(c * CHUNK, (c + 1) * CHUNK):
            finish(a)

    def take(off):
        for copy in part_copies(off):
            copy.wait_recv()
        for j in range(own_slots):
            for a in range(nb):
                mine = gy * own_slots + j
                part[mine, a] = part[mine, a] + decoded(off, j, a)

    for off in range(1, n_gy):
        take(off)
    for j in range(own_slots):
        for a in range(nb):
            total = part[gy * own_slots + j, a]
            ham_ref[j, a, :half, :] = total[:, :size]
            ham_ref[j, a, half:, :] = total[:, size:]

    for y in range(rows_y):
        x_copy(0, y).wait_send()
        x_copy(2, y).wait_send()
    both_sides(lambda side: share_copy(side).wait_send())
    both_sides(lambda side: edge_copy(side, 1, 0).wait_send())
    pl.when(gy > 1)(lambda: edge_copy(0, far, 1).wait_send())
    across(lambda side: across_copy(side).wait_send())
    for d in range(1, n_gy):
        for h in range(HALVES):
            k_sends(d, h, lambda copy: copy.wait_send())
    for c in range(chunks):
        for i in range(SWEEPS):
            both_sides(lambda side: halo_copy(side, i, c).wait_send())

    for off in range(1, n_gy):
        for copy in part_copies(off):
            copy.wait_send()


def store_body(support_ref, ham_ref, support_out, ham_out, sem):
    copies = [
        pltpu.make_async_copy(support_ref, support_out, sem.at[0]),
        pltpu.make_async_copy(ham_ref, ham_out, sem.at[1]),
    ]
    for copy in copies:
        copy.start()
    for copy in copies:
        copy.wait()


def local(n_gx, n_gy, support_funcs, potential, kernel, weighted, columns, regions):
    own_slots, nb, size = kernel.shape[:3]
    orbitals, rows_y, depth = support_funcs.shape
    slots = own_slots * n_gy
    flat = orbitals * rows_y
    chunks = nb // CHUNK
    vmem = pl.BlockSpec(memory_space=pltpu.VMEM)
    dma = pltpu.SemaphoreType.DMA
    operands = (
        columns.T, regions.T, potential, support_funcs.reshape(flat, depth), kernel, weighted
    )
    planes = [pltpu.VMEM((3 * nb, size, depth), bf16) for _ in range(rows_y)]
    parts = (slots, nb, size // 2, 2 * size)
    new_support, hamiltonian = pl.pallas_call(
        functools.partial(kernel_body, n_gx, n_gy, rows_y),
        out_shape=(
            jax.ShapeDtypeStruct((flat, depth), f32),
            jax.ShapeDtypeStruct((own_slots, nb, size, size), f32),
        ),
        in_specs=[pl.BlockSpec(memory_space=pltpu.HBM)] * 6,
        out_specs=(vmem, vmem),
        scratch_shapes=[
            pltpu.SMEM((slots, nb), jnp.int32),
            pltpu.SMEM((4, nb), jnp.int32),
            pltpu.VMEM((rows_y, depth), f32),
            pltpu.VMEM((flat, depth), bf16),
            pltpu.VMEM(kernel.shape, bf16),
            pltpu.VMEM(kernel.shape, bf16),
            pltpu.VMEM((flat, depth), f32),
            planes,
            planes,
            pltpu.VMEM((2, 3 * nb, size, depth), bf16),
            pltpu.VMEM((slots, nb, size, 2 * size), bf16),
            pltpu.VMEM((nb, rows_y, size, depth), f32),
            pltpu.VMEM((rows_y, nb, size, depth), bf16),
            pltpu.VMEM((2, SWEEPS, nb, size, depth), bf16),
            pltpu.VMEM(parts, f32),
            pltpu.VMEM(parts, jnp.int16),
            pltpu.VMEM((n_gy - 1, own_slots) + parts[1:], jnp.int16),
            pltpu.VMEM((slots, 8, 2 * size), f32),
            pltpu.VMEM((n_gy - 1, own_slots, 8, 2 * size), f32),
            dma((6,)),
            dma((3, rows_y)),
            dma((3, rows_y)),
            dma((2, 2)),
            dma((2, 2)),
            dma((2,)),
            dma((2,)),
            dma((2, n_gy - 1, HALVES)),
            dma((2, n_gy - 1, HALVES)),
            dma((2, SWEEPS, chunks)),
            dma((2, SWEEPS, chunks)),
            dma((n_gy - 1,)),
            dma((n_gy - 1,)),
            dma((n_gy - 1,)),
            dma((n_gy - 1,)),
            dma((2,)),
            dma((2,)),
        ],
        compiler_params=pltpu.CompilerParams(
            collective_id=0, has_side_effects=True, vmem_limit_bytes=40 * 1024 * 1024
        ),
    )(*[pltpu.with_memory_space_constraint(v, pltpu.HBM) for v in operands])
    hbm = pl.BlockSpec(memory_space=pltpu.HBM)
    new_support, hamiltonian = pl.pallas_call(
        store_body,
        out_shape=(
            jax.ShapeDtypeStruct(new_support.shape, f32),
            jax.ShapeDtypeStruct(hamiltonian.shape, f32),
        ),
        in_specs=[vmem, vmem],
        out_specs=(hbm, hbm),
        scratch_shapes=[dma((2,))],
        compiler_params=pltpu.CompilerParams(vmem_limit_bytes=8 * 1024 * 1024),
    )(new_support, hamiltonian)
    return (new_support.reshape(orbitals, rows_y, depth), hamiltonian)


def solution(mesh):
    return jax.shard_map(
        functools.partial(local, mesh.shape["gx"], mesh.shape["gy"]),
        mesh=mesh,
        in_specs=(
            P("gx", "gy", None),
            P("gy", None),
            P("gy", "gx", None, None),
            P("gy", "gx", None, None),
            P("gx", None),
            P("gx", None),
        ),
        out_specs=(P("gx", "gy", None), P("gy", "gx", None, None)),
        check_vma=False,
    )
```

```python
import functools

import jax
import jax.numpy as jnp
from jax import lax
from jax.experimental import pallas as pl
from jax.experimental.pallas import tpu as pltpu
from jax.sharding import PartitionSpec as P

SWEEPS = 3
CHUNK = 3
HALVES = 2
TOP = 32767.0
kinetic_cut = 1.0
step_length = 0.5
f32 = jnp.float32
bf16 = jnp.bfloat16


def remote(src, dst, send, recv, **device):
    return pltpu.make_async_remote_copy(
        src_ref=src,
        dst_ref=dst,
        send_sem=send,
        recv_sem=recv,
        device_id=device,
        device_id_type=pl.DeviceIdType.MESH,
    )


def signal(barrier, **device):
    pl.semaphore_signal(barrier, device_id=device, device_id_type=pl.DeviceIdType.MESH)


def kernel_body(
    n_gx, n_gy, rows_y,
    cols_hbm, regs_hbm, pot_hbm, x_hbm, kern_hbm, wght_hbm,
    out_ref, ham_ref,
    cols_ref, regs_ref, pot_ref, x_ref, kern_ref, wght_ref, wide, phi, app, edges, packs,
    grad, halo_out, halo_in, part, code_out, code_in, top_out, top_in, in_sem,
    x_send, x_recv, e_send, e_recv, f_send, f_recv, k_send, k_recv, g_send, g_recv,
    h_send, h_recv, t_send, t_recv, a_send, a_recv,
):
    gx, gy = lax.axis_index("gx"), lax.axis_index("gy")
    right, left = lax.rem(gx + 1, n_gx), lax.rem(gx + n_gx - 1, n_gx)
    odd = lax.rem(gx, 2)
    partner, outside = gx + 1 - 2 * odd, jnp.where(odd == 1, right, left)
    above, below = jnp.minimum(gy + 1, n_gy - 1), jnp.maximum(gy - 1, 0)
    has_low, has_high = gy > 0, gy < n_gy - 1
    near = 2 - 2 * odd
    far = 2 - near
    own_slots, nb, size = kern_ref.shape[:3]
    slots = own_slots * n_gy
    depth = x_ref.shape[1]
    brick = size * rows_y
    chunks = nb // CHUNK
    half = size // 2
    volume = 1.0 / (rows_y * n_gy * depth)
    inner, outer = tuple(range(1, rows_y - 1)), (0, rows_y - 1)

    pairs = (
        (kern_hbm, kern_ref), (wght_hbm, wght_ref), (x_hbm, x_ref),
        (pot_hbm, pot_ref), (cols_hbm, cols_ref), (regs_hbm, regs_ref),
    )
    loads = [pltpu.make_async_copy(src, dst, in_sem.at[i]) for i, (src, dst) in enumerate(pairs)]
    for load in loads:
        load.start()
    barrier = pltpu.get_barrier_semaphore()
    signal(barrier, gx=left)
    signal(barrier, gx=right)
    pl.when(has_low)(lambda: signal(barrier, gy=below))
    pl.when(has_high)(lambda: signal(barrier, gy=above))

    def both_sides(action):
        pl.when(has_low)(lambda: action(0))
        pl.when(has_high)(lambda: action(1))

    def beside(side):
        return below if side == 0 else above

    @pl.when(gy == 0)
    def _():
        edges[0] = jnp.zeros(edges.shape[1:], bf16)
        halo_in[0] = jnp.zeros(halo_in.shape[1:], bf16)

    @pl.when(gy == n_gy - 1)
    def _():
        edges[1] = jnp.zeros(edges.shape[1:], bf16)
        halo_in[1] = jnp.zeros(halo_in.shape[1:], bf16)

    def group_at(group):
        return pl.ds(group * nb, nb)

    def x_copy(group, y):
        return remote(
            phi[y].at[group_at(1)], phi[y].at[group_at(group)],
            x_send.at[group, y], x_recv.at[group, y], gx=right if isinstance(group, int) and group == 0 else left,
        )

    def k_copy(up, d, h):
        origin = gy - (d - 1) if up else gy + (d - 1)
        place = pl.ds(jnp.clip(origin, 0, n_gy - 1) * own_slots, own_slots)
        piece = pl.ds(h * (nb // HALVES), nb // HALVES)
        side = 1 if up else 0
        return remote(
            packs.at[place, piece], packs.at[place, piece],
            k_send.at[side, d - 1, h], k_recv.at[side, d - 1, h], gy=beside(side),
        )

    def k_sends(d, h, action):
        pl.when((gy - (d - 1) >= 0) & has_high)(lambda: action(k_copy(True, d, h)))
        pl.when((gy + (d - 1) < n_gy) & has_low)(lambda: action(k_copy(False, d, h)))

    def k_arrived(d, h):
        pl.when(gy - d >= 0)(lambda: k_copy(True, d, h).wait_recv())
        pl.when(gy + d < n_gy)(lambda: k_copy(False, d, h).wait_recv())

    def k_relay(d):
        for h in range(HALVES):
            k_arrived(d - 1, h)
            k_sends(d, h, lambda copy: copy.start())

    def edge_copy(side, group, index):
        y = 0 if side == 0 else rows_y - 1
        return remote(
            phi[y].at[group_at(group)], edges.at[1 - side, group_at(group)],
            e_send.at[side, index], e_recv.at[1 - side, index], gy=beside(side),
        )

    def edges_arrived(group, index):
        both_sides(lambda side: edge_copy(1 - side, group, index).wait_recv())

    def share_copy(side):
        return remote(
            edges.at[side, group_at(1)], edges.at[side, group_at(far)],
            f_send.at[side], f_recv.at[side], gx=partner,
        )

    def across_copy(side):
        return remote(
            edges.at[side, group_at(1)], edges.at[side, group_at(near)],
            a_send.at[side], a_recv.at[side], gx=outside,
        )

    def across(action):
        pl.when(gy == 0)(lambda: action(1))
        pl.when(gy > 0)(lambda: action(0))

    def across_arrived(side):
        remote(
            edges.at[side, group_at(1)], edges.at[side, group_at(far)],
            a_send.at[side], a_recv.at[side], gx=outside,
        ).wait_recv()

    def apply_rows(group, chosen):
        for i in range(nb):
            p = group * nb + i
            line = {}
            for y in sorted({y + step for y in chosen for step in (-1, 0, 1)}):
                inside = phi[y][p] if 0 <= y < rows_y else edges[0 if y < 0 else 1, p]
                line[y] = inside.astype(f32)
            for y in chosen:
                center = line[y]
                around = (
                    line[y + 1] + line[y - 1] + pltpu.roll(center, 1, 1) + pltpu.roll(center, depth - 1, 1)
                )
                applied = -0.5 * (around - 4.0 * center) + pot_ref[y : y + 1, :] * center
                app[y][p] = applied.astype(bf16)

    def picks(a):
        start = nb * n_gx + nb - nb * gx
        found = [lax.rem(cols_ref[k, a] + start, nb * n_gx) for k in range(slots)]
        return [jnp.minimum(p, 3 * nb - 1) for p in found]

    def halo_copy(side, i, c):
        y = i if side == 0 else rows_y - SWEEPS + i
        piece = pl.ds(c * CHUNK, CHUNK)
        return remote(
            halo_out.at[y, piece], halo_in.at[1 - side, i, piece],
            g_send.at[side, i, c], g_recv.at[1 - side, i, c], gy=beside(side),
        )

    def gradient_of(chosen):
        for a in range(nb):
            where = picks(a)
            mixing = jnp.concatenate([packs[k, a] for k in range(slots)], axis=1)
            source = jnp.concatenate(
                [
                    jnp.concatenate([v for p in where for v in (app[y][p], phi[y][p])], axis=0)
                    for y in chosen
                ],
                axis=1,
            )
            total = jnp.dot(mixing, source, preferred_element_type=f32)
            for j, y in enumerate(chosen):
                piece = total[:, j * depth : (j + 1) * depth]
                grad[a, y] = piece
                halo_out[y, a] = piece.astype(bf16)
            if a % CHUNK == CHUNK - 1:
                for y in chosen:
                    if y < SWEEPS:
                        pl.when(has_low)(lambda: halo_copy(0, y, a // CHUNK).start())
                    if y >= rows_y - SWEEPS:
                        pl.when(has_high)(
                            lambda: halo_copy(1, y - rows_y + SWEEPS, a // CHUNK).start()
                        )

    def part_of(a):
        def whole(block, p):
            return jnp.concatenate([block[y][p] for y in range(rows_y)], axis=1)

        source = jnp.concatenate([whole(app, p) for p in picks(a)], axis=0)
        block = lax.dot_general(
            whole(phi, nb + a), source, (((1,), (1,)), ((), ())), preferred_element_type=f32
        ) * volume
        for k in range(slots):
            one = block[:, k * size : (k + 1) * size]
            part[k, a] = jnp.concatenate([one[:half], one[half:]], axis=1)

    def split(value):
        return [value[i : i + 8] for i in range(0, half, 8)]

    def encode(s):
        for j in range(own_slots):
            spot = s * own_slots + j
            top = jnp.full((8, 2 * size), 1e-33, f32)
            for a in range(nb):
                for value in split(part[spot, a]):
                    top = jnp.maximum(top, jnp.abs(value))
            top_out[spot] = top
            scale = TOP / top
            for a in range(nb):
                coded = jnp.concatenate([value * scale for value in split(part[spot, a])], axis=0)
                code_out[spot, a] = jnp.round(coded).astype(jnp.int32).astype(jnp.int16)

    def decoded(off, j, a):
        step = top_in[off - 1, j] * (1.0 / TOP)
        coded = code_in[off - 1, j, a].astype(jnp.int32).astype(f32)
        return jnp.concatenate([value * step for value in split(coded)], axis=0)

    def part_copies(off):
        peer = lax.rem(gy + off, n_gy)
        place = pl.ds(peer * own_slots, own_slots)
        return (
            remote(
                top_out.at[place], top_in.at[off - 1], t_send.at[off - 1], t_recv.at[off - 1], gy=peer
            ),
            remote(
                code_out.at[place], code_in.at[off - 1], h_send.at[off - 1], h_recv.at[off - 1], gy=peer
            ),
        )

    def pass_on(off):
        encode(lax.rem(gy + off, n_gy))
        for copy in part_copies(off):
            copy.start()

    diag = 1.0 + 2.0 / kinetic_cut
    coef = 0.5 / kinetic_cut
    low, high = jnp.where(has_low, 1.0, 0.0).astype(f32), jnp.where(has_high, 1.0, 0.0).astype(f32)
    z_index = lax.broadcasted_iota(jnp.int32, (size, depth), 1)

    def finish(a):
        field = [halo_in[0, i, a].astype(f32) for i in range(SWEEPS)]
        field += [grad[a, y] for y in range(rows_y)]
        field += [halo_in[1, i, a].astype(f32) for i in range(SWEEPS)]
        field = [value * (1.0 / diag) for value in field]
        now = list(field)
        for sweep in range(1, SWEEPS + 1):
            later = list(now)
            for i in range(sweep, rows_y + 2 * SWEEPS - sweep):
                around = now[i - 1] + now[i + 1]
                around = around + pltpu.roll(now[i], 1, 1) + pltpu.roll(now[i], depth - 1, 1)
                value = field[i] + (coef / diag) * around
                if i < SWEEPS:
                    value = value * low
                if i >= rows_y + SWEEPS:
                    value = value * high
                later[i] = value
            now = later
        z_in = (z_index >= regs_ref[2, a]) & (z_index < regs_ref[3, a])
        for y in range(rows_y):
            spot = gy * rows_y + y
            y_in = jnp.where((spot >= regs_ref[0, a]) & (spot < regs_ref[1, a]), step_length, 0.0)
            masked = jnp.where(z_in, now[SWEEPS + y] * y_in.astype(f32), 0.0)
            out_ref[pl.ds(a * brick + y, size, stride=rows_y), :] = phi[y][nb + a].astype(f32) - masked

    loads[0].wait()
    loads[1].wait()
    for j in range(own_slots):
        for a in range(nb):
            packs[gy * own_slots + j, a] = jnp.concatenate([kern_ref[j, a], -wght_ref[j, a]], axis=1)
    loads[2].wait()
    wide[...] = x_ref[...].astype(f32)

    pl.semaphore_wait(barrier, 2 + has_low.astype(jnp.int32) + has_high.astype(jnp.int32))
    for h in range(HALVES):
        k_sends(1, h, lambda copy: copy.start())
    for y in range(rows_y):
        for a in range(nb):
            phi[y][nb + a] = wide[pl.ds(a * brick + y, size, stride=rows_y), :].astype(bf16)
        x_copy(0, y).start()
        x_copy(2, y).start()
    both_sides(lambda side: edge_copy(side, 1, 0).start())
    for load in loads[3:]:
        load.wait()
    apply_rows(1, inner)
    if n_gy > 2:
        k_relay(2)
    for y in range(rows_y):
        x_copy(near, y).wait_recv()
    apply_rows(near, inner)
    x_copy(far, 0).wait_recv()
    pl.when(gy > 1)(lambda: edge_copy(0, far, 1).start())
    for d in range(3, n_gy):
        k_relay(d)
    x_copy(far, 1).wait_recv()
    for y in inner:
        x_copy(far, y + 1).wait_recv()
        apply_rows(far, (y,))
        if y == inner[0]:
            for h in range(HALVES):
                k_arrived(n_gy - 1, h)
        gradient_of((y,))
        if y == inner[0]:
            edges_arrived(1, 0)
            across(lambda side: across_copy(side).start())
            both_sides(lambda side: share_copy(side).start())
            apply_rows(1, outer)
    both_sides(lambda side: share_copy(side).wait_recv())
    apply_rows(near, outer)
    pl.when(gy == 0)(lambda: across_arrived(1))
    pl.when((gy > 0) & has_high)(lambda: edge_copy(0, far, 1).wait_recv())
    apply_rows(far, outer[1:])
    gradient_of(outer[1:])
    pl.when(gy > 0)(lambda: across_arrived(0))
    apply_rows(far, outer[:1])
    for a in range(nb):
        part_of(a)
    gradient_of(outer[:1])
    for i in range(1, n_gy):
        pass_on(jnp.where(gy < n_gy // 2, n_gy - i, i))
    for c in range(chunks):
        for i in range(SWEEPS):
            both_sides(lambda side: halo_copy(1 - side, i, c).wait_recv())
        for a in range(c * CHUNK, (c + 1) * CHUNK):
            finish(a)

    def take(off):
        for copy in part_copies(off):
            copy.wait_recv()
        for j in range(own_slots):
            for a in range(nb):
                mine = gy * own_slots + j
                part[mine, a] = part[mine, a] + decoded(off, j, a)

    for off in range(1, n_gy):
        take(off)
    for j in range(own_slots):
        for a in range(nb):
            total = part[gy * own_slots + j, a]
            ham_ref[j, a, :half, :] = total[:, :size]
            ham_ref[j, a, half:, :] = total[:, size:]

    for y in range(rows_y):
        x_copy(0, y).wait_send()
        x_copy(2, y).wait_send()
    both_sides(lambda side: share_copy(side).wait_send())
    both_sides(lambda side: edge_copy(side, 1, 0).wait_send())
    pl.when(gy > 1)(lambda: edge_copy(0, far, 1).wait_send())
    across(lambda side: across_copy(side).wait_send())
    for d in range(1, n_gy):
        for h in range(HALVES):
            k_sends(d, h, lambda copy: copy.wait_send())
    for c in range(chunks):
        for i in range(SWEEPS):
            both_sides(lambda side: halo_copy(side, i, c).wait_send())

    for off in range(1, n_gy):
        for copy in part_copies(off):
            copy.wait_send()


def store_body(support_ref, ham_ref, support_out, ham_out, sem):
    copies = [
        pltpu.make_async_copy(support_ref, support_out, sem.at[0]),
        pltpu.make_async_copy(ham_ref, ham_out, sem.at[1]),
    ]
    for copy in copies:
        copy.start()
    for copy in copies:
        copy.wait()


def local(n_gx, n_gy, support_funcs, potential, kernel, weighted, columns, regions):
    own_slots, nb, size = kernel.shape[:3]
    orbitals, rows_y, depth = support_funcs.shape
    slots = own_slots * n_gy
    flat = orbitals * rows_y
    chunks = nb // CHUNK
    vmem = pl.BlockSpec(memory_space=pltpu.VMEM)
    dma = pltpu.SemaphoreType.DMA
    operands = (
        columns.T, regions.T, potential, support_funcs.reshape(flat, depth), kernel, weighted
    )
    planes = [pltpu.VMEM((3 * nb, size, depth), bf16) for _ in range(rows_y)]
    parts = (slots, nb, size // 2, 2 * size)
    new_support, hamiltonian = pl.pallas_call(
        functools.partial(kernel_body, n_gx, n_gy, rows_y),
        out_shape=(
            jax.ShapeDtypeStruct((flat, depth), f32),
            jax.ShapeDtypeStruct((own_slots, nb, size, size), f32),
        ),
        in_specs=[pl.BlockSpec(memory_space=pltpu.HBM)] * 6,
        out_specs=(vmem, vmem),
        scratch_shapes=[
            pltpu.SMEM((slots, nb), jnp.int32),
            pltpu.SMEM((4, nb), jnp.int32),
            pltpu.VMEM((rows_y, depth), f32),
            pltpu.VMEM((flat, depth), bf16),
            pltpu.VMEM(kernel.shape, bf16),
            pltpu.VMEM(kernel.shape, bf16),
            pltpu.VMEM((flat, depth), f32),
            planes,
            planes,
            pltpu.VMEM((2, 3 * nb, size, depth), bf16),
            pltpu.VMEM((slots, nb, size, 2 * size), bf16),
            pltpu.VMEM((nb, rows_y, size, depth), f32),
            pltpu.VMEM((rows_y, nb, size, depth), bf16),
            pltpu.VMEM((2, SWEEPS, nb, size, depth), bf16),
            pltpu.VMEM(parts, f32),
            pltpu.VMEM(parts, jnp.int16),
            pltpu.VMEM((n_gy - 1, own_slots) + parts[1:], jnp.int16),
            pltpu.VMEM((slots, 8, 2 * size), f32),
            pltpu.VMEM((n_gy - 1, own_slots, 8, 2 * size), f32),
            dma((6,)),
            dma((3, rows_y)),
            dma((3, rows_y)),
            dma((2, 2)),
            dma((2, 2)),
            dma((2,)),
            dma((2,)),
            dma((2, n_gy - 1, HALVES)),
            dma((2, n_gy - 1, HALVES)),
            dma((2, SWEEPS, chunks)),
            dma((2, SWEEPS, chunks)),
            dma((n_gy - 1,)),
            dma((n_gy - 1,)),
            dma((n_gy - 1,)),
            dma((n_gy - 1,)),
            dma((2,)),
            dma((2,)),
        ],
        compiler_params=pltpu.CompilerParams(
            collective_id=0, has_side_effects=True, vmem_limit_bytes=40 * 1024 * 1024
        ),
    )(*[pltpu.with_memory_space_constraint(v, pltpu.HBM) for v in operands])
    hbm = pl.BlockSpec(memory_space=pltpu.HBM)
    new_support, hamiltonian = pl.pallas_call(
        store_body,
        out_shape=(
            jax.ShapeDtypeStruct(new_support.shape, f32),
            jax.ShapeDtypeStruct(hamiltonian.shape, f32),
        ),
        in_specs=[vmem, vmem],
        out_specs=(hbm, hbm),
        scratch_shapes=[dma((2,))],
        compiler_params=pltpu.CompilerParams(vmem_limit_bytes=8 * 1024 * 1024),
    )(new_support, hamiltonian)
    return (new_support.reshape(orbitals, rows_y, depth), hamiltonian)


def solution(mesh):
    return jax.shard_map(
        functools.partial(local, mesh.shape["gx"], mesh.shape["gy"]),
        mesh=mesh,
        in_specs=(
            P("gx", "gy", None),
            P("gy", None),
            P("gy", "gx", None, None),
            P("gy", "gx", None, None),
            P("gx", None),
            P("gx", None),
        ),
        out_specs=(P("gx", "gy", None), P("gy", "gx", None, None)),
        check_vma=False,
    )
```
